32 devices in a mesh: layer: 4 (over x, core), feat: 4 (over z), par: 2 (over y).
Axes of the slice: x: 2, y: 2, z: 4, core: 2. Of those that a mesh axis runs over, the one named last changes fastest.
Arguments:
- residual: bfloat16 [4, 512, 2304], P('layer'), may hold values from -6 to 6
- norm_gain: float32 [4, 2304], P('layer'), may hold values from 0.5 to 1.5
- gate_weight: bfloat16 [4, 2304, 9216], P('layer', None, ('feat', 'par')), may hold values from -0.125 to 0.125
- up_weight: bfloat16 [4, 2304, 9216], P('layer', None, ('feat', 'par')), may hold values from -0.125 to 0.125
- down_weight: bfloat16 [4, 9216, 2304], P('layer', ('feat', 'par')), may hold values from -0.0625 to 0.0625
- enc_weight: float32 [4, 2304, 8192], P('layer', 'par', 'feat'), may hold values from -0.125 to 0.125
- enc_bias: float32 [4, 8192], P('layer', 'feat'), may hold values from -1 to 0.5
- dec_weight: bfloat16 [4, 2, 2, 8192, 2304], P('layer', 'par', None, 'feat'), may hold values from -0.0625 to 0.0625
- dec_bias: float32 [4, 2304], replicated, may hold values from -3 to 3
Outputs:
- enc_grad: float32 [4, 2304, 8192], P('layer', 'par', 'feat')
- enc_bias_grad: float32 [4, 8192], P('layer', 'feat')
- dec_grad: bfloat16 [4, 2, 2, 8192, 2304], P('layer', 'par', None, 'feat')
The draws below stay inside these ranges and needn't reach their ends.
All inputs are finite; a program needn't handle non-finite values.
Results may differ from the reference program's by a relative error of at most 0.007.
Values may be sent and summed in bfloat16 or wider, within the bound.
No kernel may reach another device: no remote copies, remote signals or barrier semaphores. Data moves between devices by JAX's collectives and lax.ppermute only.
A program may use at most 192 MiB of HBM per device.

```python
import jax
import jax.numpy as jnp
from jax import lax

D = 2304
FF = 9216
FEATS = 8192
LAYERS = 4
TOKENS = 512


def block_levels(own_key, dims, pieces, low, high):
    factor_of, own = 1.0, jax.random.fold_in(own_key, 6)
    for dim, blocks in pieces:
        draws = jnp.exp(jax.random.uniform(jax.random.fold_in(own, dim), (blocks,), jnp.float32, low / len(pieces), high / len(pieces)))
        factor_of = factor_of * jnp.repeat(draws, dims[dim] // blocks).reshape([-1 if axis == dim else 1 for axis in range(len(dims))])
    return factor_of


def bell_draw(key, shape, scale, reach, split=(), dtype=jnp.bfloat16):
    entries = jax.random.normal(key, shape, jnp.float32) * scale
    if len(split) > 0:
        entries = block_levels(key, shape, split, -0.22, 0.18) * entries
    return jnp.clip(entries, min=-reach, max=reach).astype(dtype)


def setup_inputs(seed: int = 0) -> dict:
    streams_of = jax.random.split(jax.random.key(seed), 10)
    residual = bell_draw(streams_of[0], (LAYERS, TOKENS, D), 1.0, 6.0, ((0, 4),))
    norm_gain = jnp.clip(1.0 + 0.1 * jax.random.normal(streams_of[1], (LAYERS, D), jnp.float32), 0.5, 1.5)
    gate_weight = bell_draw(streams_of[2], (LAYERS, D, FF), D ** -0.5, 0.125, ((0, 4), (2, 8)))
    up_weight = bell_draw(streams_of[3], (LAYERS, D, FF), D ** -0.5, 0.125, ((0, 4), (2, 8)))
    down_weight = bell_draw(streams_of[4], (LAYERS, FF, D), FF ** -0.5, 0.0625, ((0, 4), (1, 8)))
    enc_weight = bell_draw(streams_of[5], (LAYERS, D, FEATS), D ** -0.5, 0.125, ((0, 4), (1, 2), (2, 4)), jnp.float32)
    enc_bias = jnp.clip(-1.0 + 1.5 * jax.random.uniform(streams_of[6], (LAYERS, FEATS), jnp.float32) ** block_levels(streams_of[6], (LAYERS, FEATS), ((0, 4), (1, 4)), -0.2, 0.2), -1.0, 0.5)
    dec_weight = bell_draw(streams_of[7], (LAYERS, 2, LAYERS // 2, FEATS, D), FEATS ** -0.5, 0.0625, ((0, 4), (1, 2), (3, 4)))
    dec_bias = bell_draw(streams_of[8], (LAYERS, D), 0.5, 3.0, (), jnp.float32)
    return {"residual": residual, "norm_gain": norm_gain, "gate_weight": gate_weight, "up_weight": up_weight, "down_weight": down_weight, "enc_weight": enc_weight, "enc_bias": enc_bias, "dec_weight": dec_weight, "dec_bias": dec_bias}


def rms_normed(rows_in, gain_row):
    values = rows_in.astype(jnp.float32)
    scaling = lax.rsqrt(lax.optimization_barrier(jnp.mean(values * values, axis=-1, keepdims=True)) + 1e-06)
    return (values * scaling * gain_row).astype(jnp.bfloat16)

def reference(residual, norm_gain, gate_weight, up_weight, down_weight, enc_weight, enc_bias, dec_weight, dec_bias):
    highest = lax.Precision.HIGHEST
    normed = []
    targets = []
    positives = []
    actives = []
    for source in range(LAYERS):
        rows_in = rms_normed(residual[source], norm_gain[source])
        gate_value = jnp.dot(rows_in, gate_weight[source], preferred_element_type=jnp.float32)
        up_value = jnp.dot(rows_in, up_weight[source], preferred_element_type=jnp.float32)
        hidden = (jax.nn.gelu(gate_value, approximate=True) * up_value).astype(jnp.bfloat16)
        targets.append(jnp.dot(hidden, down_weight[source], preferred_element_type=jnp.float32))
        pre_act = jnp.dot(rows_in.astype(jnp.float32), enc_weight[source], precision=highest) + enc_bias[source]
        positive = jnp.maximum(pre_act, 0.0)
        normed.append(rows_in)
        positives.append(positive)
        actives.append((positive * positive).astype(jnp.bfloat16))
    errors = []
    for target in range(LAYERS):
        summed_rows = jnp.zeros((TOKENS, D), jnp.float32)
        for source in range(target + 1):
            summed_rows = summed_rows + jnp.dot(actives[source], dec_weight[source, target % 2, target // 2], preferred_element_type=jnp.float32)
        errors.append(((summed_rows + dec_bias[target] - targets[target]) * 0.0625).astype(jnp.bfloat16))
    enc_grads = []
    bias_grads = []
    dec_grads = []
    zero_block = jnp.zeros((FEATS, D), jnp.bfloat16)
    for source in range(LAYERS):
        back_grad = jnp.zeros((TOKENS, FEATS), jnp.float32)
        for parity in range(2):
            for slot_index in range(LAYERS // 2):
                target = 2 * slot_index + parity
                if target >= source:
                    back_grad = back_grad + lax.dot_general(errors[target], dec_weight[source, parity, slot_index], (((1,), (1,)), ((), ())), preferred_element_type=jnp.float32)
                    dec_grads.append(lax.dot_general(actives[source], errors[target], (((0,), (0,)), ((), ())), preferred_element_type=jnp.float32).astype(jnp.bfloat16))
                else:
                    dec_grads.append(zero_block)
        d_pre = back_grad * 2.0 * positives[source]
        enc_grads.append(lax.dot_general(normed[source].astype(jnp.float32), d_pre, (((0,), (0,)), ((), ())), precision=highest))
        bias_grads.append(lax.optimization_barrier(jnp.sum(d_pre, axis=0)))
    dec_grad = jnp.stack(dec_grads).reshape(LAYERS, 2, LAYERS // 2, FEATS, D)
    return (jnp.stack(enc_grads), jnp.stack(bias_grads), dec_grad)
```

```python
import functools

import jax
import jax.numpy as jnp
from jax import lax
from jax.experimental import pallas as pl
from jax.experimental.pallas import tpu as pltpu
from jax.sharding import PartitionSpec as P


CHUNKS = 2
F32 = jnp.float32
BF16 = jnp.bfloat16
LIMITS = pltpu.CompilerParams(vmem_limit_bytes=46 * 2**20)


def tile_of(size, limit):
    best = size
    for tile in range(128, min(size, limit) + 1, 128):
        if size % tile == 0:
            best = tile
    return best


def positive_of(own, moved, bias):
    return jnp.maximum(own.astype(F32) + moved.astype(F32) + bias, 0.0)


def tied(value, *first):
    return lax.optimization_barrier((value, *first))[0]


def product(left, right, left_dim, right_dim):
    return lax.dot_general(
        left, right, (((left_dim,), (right_dim,)), ((), ())), preferred_element_type=F32
    )


def encode_body(place_ref, rows_ref, gain_ref, weight_ref, normed_ref, *rest):
    send_refs, half_ref = rest[:-1], rest[-1]
    blocks = place_ref.shape[0] - 1
    tokens, half = half_ref.shape
    size = tokens // blocks

    @pl.when(pl.program_id(0) == 0)
    def _():
        column = pl.multiple_of(place_ref[blocks] * half, 128)
        for b in range(blocks):
            start = pl.multiple_of(place_ref[b] * size, size)
            values = rows_ref[pl.ds(start, size), :].astype(F32)
            scaling = lax.rsqrt(jnp.mean(values * values, axis=-1, keepdims=True) + 1e-06)
            kept = slice(b * size, (b + 1) * size)
            normed_ref[kept, :] = (values * scaling * gain_ref[...]).astype(BF16)
            half_ref[kept, :] = normed_ref[kept, pl.ds(column, half)]

    part = product(half_ref[...], weight_ref[...].astype(BF16), 1, 0)
    span = tokens // len(send_refs)
    for c, send_ref in enumerate(send_refs):
        send_ref[...] = part[c * span : (c + 1) * span].astype(BF16)


def encode(place, rows, gain, weight):
    tokens, width = rows.shape
    half, feats = weight.shape
    tile = tile_of(feats, 512)
    size = tokens // CHUNKS
    return pl.pallas_call(
        encode_body,
        grid_spec=pltpu.PrefetchScalarGridSpec(
            num_scalar_prefetch=1,
            grid=(feats // tile,),
            in_specs=[
                pl.BlockSpec((tokens, width), lambda f, place: (0, 0)),
                pl.BlockSpec((1, width), lambda f, place: (0, 0)),
                pl.BlockSpec((half, tile), lambda f, place: (0, f)),
            ],
            out_specs=[pl.BlockSpec((tokens, width), lambda f, place: (0, 0))]
            + [pl.BlockSpec((size, tile), lambda f, place: (0, f))] * CHUNKS,
            scratch_shapes=[pltpu.VMEM((tokens, half), BF16)],
        ),
        out_shape=[jax.ShapeDtypeStruct((tokens, width), BF16)]
        + [jax.ShapeDtypeStruct((size, feats), BF16)] * CHUNKS,
        name="encode",
    )(place, rows, gain, weight)


def mlp_body(k_steps, rows_ref, gate_ref, up_ref, down_ref, out_ref, gate_acc, up_acc, hidden):
    step = pl.program_id(0)

    @pl.when(step == 0)
    def _():
        gate_acc[...] = product(rows_ref[...], gate_ref[...], 1, 0)
        up_acc[...] = product(rows_ref[...], up_ref[...], 1, 0)

    @pl.when((step > 0) & (step < k_steps))
    def _():
        gate_acc[...] += product(rows_ref[...], gate_ref[...], 1, 0)
        up_acc[...] += product(rows_ref[...], up_ref[...], 1, 0)

    @pl.when(step == k_steps - 1)
    def _():
        hidden[...] = (jax.nn.gelu(gate_acc[...], approximate=True) * up_acc[...]).astype(BF16)

    @pl.when(step >= k_steps)
    def _():
        out_ref[...] = product(hidden[...], down_ref[...], 1, 0).astype(BF16)


def mlp(normed, gate, up, down):
    tokens, width = normed.shape
    inner = gate.shape[1]
    tile = tile_of(width, 768)
    steps = width // tile
    early = lambda i: jnp.minimum(i, steps - 1)
    late = lambda i: jnp.maximum(i - steps, 0)
    return pl.pallas_call(
        functools.partial(mlp_body, steps),
        grid=(2 * steps,),
        in_specs=[
            pl.BlockSpec((tokens, tile), lambda i: (0, early(i))),
            pl.BlockSpec((tile, inner), lambda i: (early(i), 0)),
            pl.BlockSpec((tile, inner), lambda i: (early(i), 0)),
            pl.BlockSpec((inner, tile), lambda i: (0, late(i))),
        ],
        out_specs=pl.BlockSpec((tokens, tile), lambda i: (0, late(i))),
        out_shape=jax.ShapeDtypeStruct((tokens, width), BF16),
        scratch_shapes=[
            pltpu.VMEM((tokens, inner), F32),
            pltpu.VMEM((tokens, inner), F32),
            pltpu.VMEM((tokens, inner), BF16),
        ],
        name="mlp",
    )(normed, gate, up, down)


def decode_body(
    flags_ref, own_ref, moved_ref, bias_ref, weight_ref, target_ref, act_ref, keep_ref, send_ref
):
    slot = pl.program_id(0)
    slots = pl.num_programs(0)

    @pl.when((slot == 0) & (pl.program_id(1) == 0))
    def _():
        positive = positive_of(own_ref[...], moved_ref[...], bias_ref[...])
        act_ref[...] = (positive * positive).astype(BF16)

    live = flags_ref[slot].astype(F32)
    mine = flags_ref[slots + slot].astype(F32)
    recon = product(act_ref[...], weight_ref[0], 1, 0) * live
    recon = recon - target_ref[...].astype(F32) * mine
    half = recon.shape[0] // 2
    keep_ref[0] = recon[:half]
    send_ref[0] = recon[half:].astype(BF16)


def decode(flags, own, moved, bias, decoders, target, chunk):
    size, feats = own.shape
    slots, _, width = decoders.shape
    tile = tile_of(width, 768)
    whole = pl.BlockSpec((size, feats), lambda j, d, flags: (0, 0))
    part = pl.BlockSpec((1, size // 2, tile), lambda j, d, flags: (j, 0, d))
    return pl.pallas_call(
        decode_body,
        grid_spec=pltpu.PrefetchScalarGridSpec(
            num_scalar_prefetch=1,
            grid=(slots, width // tile),
            in_specs=[
                whole,
                whole,
                pl.BlockSpec((1, feats), lambda j, d, flags: (0, 0)),
                pl.BlockSpec((1, feats, tile), lambda j, d, flags: (j, 0, d)),
                pl.BlockSpec((size, tile), lambda j, d, flags: (chunk, d)),
            ],
            out_specs=[whole, part, part],
        ),
        out_shape=[
            jax.ShapeDtypeStruct((size, feats), BF16),
            jax.ShapeDtypeStruct((slots, size // 2, width), F32),
            jax.ShapeDtypeStruct((slots, size // 2, width), BF16),
        ],
        compiler_params=LIMITS,
        name="decode",
    )(flags, own, moved, bias, decoders, target)


def back_body(err_ref, weight_ref, part_ref, send_ref):
    part = product(err_ref[0], weight_ref[0], 1, 1)
    for j in range(1, err_ref.shape[0]):
        part = part + product(err_ref[j], weight_ref[j], 1, 1)
    part_ref[...] = part
    send_ref[...] = part.astype(BF16)


def back_product(errors, decoders):
    slots, size, width = errors.shape
    feats = decoders.shape[1]
    tile = tile_of(feats, 512)
    return pl.pallas_call(
        back_body,
        grid=(feats // tile,),
        in_specs=[
            pl.BlockSpec((slots, size, width), lambda f: (0, 0, 0)),
            pl.BlockSpec((slots, tile, width), lambda f: (0, f, 0)),
        ],
        out_specs=[
            pl.BlockSpec((size, tile), lambda f: (0, f)),
            pl.BlockSpec((size, tile), lambda f: (0, f)),
        ],
        out_shape=[
            jax.ShapeDtypeStruct((size, feats), F32),
            jax.ShapeDtypeStruct((size, feats), BF16),
        ],
        compiler_params=LIMITS,
        name="back_product",
    )(errors, decoders)


def dec_grad_body(*refs):
    acts, errs, out_ref = refs[:CHUNKS], refs[CHUNKS : 2 * CHUNKS], refs[-1]
    turned = [act_ref[...].T for act_ref in acts]
    for j in range(out_ref.shape[0]):
        total = product(turned[0], errs[0][j], 1, 0)
        for c in range(1, CHUNKS):
            total = total + product(turned[c], errs[c][j], 1, 0)
        out_ref[j] = total.astype(BF16)


def dec_grad_product(actives, errors):
    size, feats = actives[0].shape
    slots, _, width = errors[0].shape
    tile = tile_of(feats, 256)
    return pl.pallas_call(
        dec_grad_body,
        grid=(feats // tile,),
        in_specs=[pl.BlockSpec((size, tile), lambda f: (0, f))] * CHUNKS
        + [pl.BlockSpec((slots, size, width), lambda f: (0, 0, 0))] * CHUNKS,
        out_specs=pl.BlockSpec((slots, tile, width), lambda f: (0, f, 0)),
        out_shape=jax.ShapeDtypeStruct((slots, feats, width), BF16),
        compiler_params=LIMITS,
        name="dec_grad",
    )(*actives, *errors)


def enc_grad_body(parity_ref, rows_ref, bias_in_ref, *refs):
    parts, moved, own, seen = (refs[i * CHUNKS : (i + 1) * CHUNKS] for i in range(4))
    grad_ref, bias_ref = refs[-2:]
    grads = []
    bias = 0.0
    for c in range(CHUNKS):
        positive = positive_of(own[c][...], seen[c][...], bias_in_ref[...])
        d_pre = (parts[c][...] + moved[c][...].astype(F32)) * 2.0 * positive
        bias = bias + jnp.sum(d_pre, axis=0, keepdims=True)
        grads.append(d_pre.astype(BF16))
    bias_ref[...] = bias
    grad_ref[...] = product(rows_ref[...], jnp.concatenate(grads, axis=0), 0, 0)


def enc_grad_product(parity, normed, half, bias, parts, moved, own, seen):
    tokens = normed.shape[0]
    size, feats = parts[0].shape
    tile = tile_of(feats, 512)
    return pl.pallas_call(
        enc_grad_body,
        grid_spec=pltpu.PrefetchScalarGridSpec(
            num_scalar_prefetch=1,
            grid=(feats // tile,),
            in_specs=[
                pl.BlockSpec((tokens, half), lambda f, par: (0, par[0])),
                pl.BlockSpec((1, tile), lambda f, par: (0, f)),
            ]
            + [pl.BlockSpec((size, tile), lambda f, par: (0, f))] * (4 * CHUNKS),
            out_specs=[
                pl.BlockSpec((half, tile), lambda f, par: (0, f)),
                pl.BlockSpec((1, tile), lambda f, par: (0, f)),
            ],
        ),
        out_shape=[
            jax.ShapeDtypeStruct((half, feats), F32),
            jax.ShapeDtypeStruct((1, feats), F32),
        ],
        compiler_params=LIMITS,
        name="enc_grad",
    )(parity, normed, bias, *parts, *moved, *own, *seen)


def shards(
    residual,
    norm_gain,
    gate_weight,
    up_weight,
    down_weight,
    enc_weight,
    enc_bias,
    dec_weight,
    dec_bias,
):
    layers = lax.axis_size("layer")
    feat_n = lax.axis_size("feat")
    outer = layers // 2
    source = lax.axis_index("layer")
    parity = lax.axis_index("par")
    slots = dec_weight.shape[2]
    _, tokens, width = residual.shape
    half_width = enc_weight.shape[1]
    size = tokens // CHUNKS
    rows_n = size // (layers * feat_n)

    def over_par(value):
        return lax.ppermute(value, "par", [(0, 1), (1, 0)])

    def over_layer(value, mask):
        return lax.ppermute(value, "layer", [(s, s ^ mask) for s in range(layers)])

    def over_feat(value):
        return lax.all_to_all(value, "feat", 0, 0, tiled=True)

    index = jnp.arange(CHUNKS * layers, dtype=jnp.int32)
    table = index ^ (source % 2 * outer + source // 2)
    parity_arg = jnp.full((1,), parity, jnp.int32)
    place = jnp.concatenate([table, parity_arg])
    normed, *pre_send = encode(place, residual[0], norm_gain, enc_weight[0])
    pre_moved = []
    for c in range(CHUNKS):
        pre_moved.append(over_par(pre_send[c]))
    target_part = mlp(normed, gate_weight[0], up_weight[0], down_weight[0])

    pairs = [(s * 2 + 1 - s % 2, (s ^ 1) * 2 + 1 - s % 2) for s in range(layers)]
    halves = target_part.reshape(CHUNKS, 2, outer, feat_n, rows_n, width)
    handed = lax.ppermute(halves[:, 1], ("layer", "par"), pairs)
    moving = jnp.where(source % 2 == parity, handed, halves[:, 0])
    moving = moving.transpose(2, 0, 1, 3, 4)
    target_moved = over_feat(moving)

    slot_ids = jnp.arange(slots, dtype=jnp.int32)
    decoders = dec_weight[0, 0]
    live = 2 * slot_ids + parity >= source
    mine = (slot_ids == source // 2) & (source % 2 == parity)
    flags = jnp.concatenate([live, mine]).astype(jnp.int32)
    bias_rows = lax.dynamic_index_in_dim(
        dec_bias.reshape(slots, 2, width), parity, 1, keepdims=False
    )

    actives = []
    wholes = []
    last = moving
    for c in range(CHUNKS):
        active, keep, send = decode(
            flags, pre_send[c], tied(pre_moved[c], last), enc_bias, decoders, target_part, c
        )
        actives.append(active)
        got = over_layer(send, 1)
        both = (keep + got.astype(F32)).reshape(slots, outer, feat_n * rows_n, width)
        whole = both[:, 0]
        for high in range(1, outer):
            last = both[:, high].astype(BF16)
            got = over_layer(last, 2 * high)
            whole = whole + got.astype(F32)
        wholes.append(whole.astype(BF16).reshape(slots, feat_n, rows_n, width).swapaxes(0, 1))

    summed = jnp.sum(tied(target_moved, last).astype(F32), axis=0)
    crossed = over_par(summed.astype(BF16).transpose(1, 0, 2, 3))
    far_target = 0.0
    for high in range(outer):
        got = crossed[0] if high == 0 else over_layer(crossed[high], 2 * high)
        chosen = slot_ids == ((source // 2) ^ high)
        far_target = far_target + jnp.where(
            chosen[:, None, None, None], got[None].astype(F32), 0.0
        )

    gathered = []
    for c in range(CHUNKS):
        got = over_feat(wholes[c])
        if c:
            got = tied(got, error)
        total = jnp.sum(got.astype(F32), axis=0)
        error = (total - far_target[:, c] + bias_rows[:, None]) * 0.0625
        error = error.astype(BF16)
        gathered.append(over_feat(jnp.broadcast_to(error[None], (feat_n,) + error.shape)))

    errors = []
    parts = []
    moved = []
    for c in range(CHUNKS):
        rows = [gathered[c]]
        for high in range(1, outer):
            rows.append(over_layer(gathered[c], 2 * high))
        rows = jnp.stack(rows)
        other = over_layer(rows, 1)
        if c:
            rows, other = lax.optimization_barrier((rows, other, parts[-1]))[:2]
        rows = jnp.stack([rows, other])
        rows = rows.transpose(3, 0, 1, 2, 4, 5).reshape(slots, size, width)
        errors.append(jnp.where(live[:, None, None], rows, jnp.zeros_like(rows)))
        part, send = back_product(errors[c], decoders)
        parts.append(part)
        moved.append(over_par(send))
    dec_grad = dec_grad_product(actives, errors[:-1] + [tied(errors[-1], send)])
    enc_grad, bias_grad = enc_grad_product(
        parity_arg, normed, half_width, enc_bias, parts, moved, pre_send, pre_moved
    )
    return (enc_grad[None], bias_grad, dec_grad[None, None])


def solution(mesh):
    return jax.shard_map(
        shards,
        mesh=mesh,
        in_specs=(
            P("layer", None, None),
            P("layer", None),
            P("layer", None, ("feat", "par")),
            P("layer", None, ("feat", "par")),
            P("layer", ("feat", "par"), None),
            P("layer", "par", "feat"),
            P("layer", "feat"),
            P("layer", "par", None, "feat", None),
            P(),
        ),
        out_specs=(
            P("layer", "par", "feat"),
            P("layer", "feat"),
            P("layer", "par", None, "feat", None),
        ),
        check_vma=False,
    )
```

```python
import functools

import jax
import jax.numpy as jnp
from jax import lax
from jax.experimental import pallas as pl
from jax.experimental.pallas import tpu as pltpu
from jax.sharding import PartitionSpec as P


CHUNKS = 2
F32 = jnp.float32
BF16 = jnp.bfloat16
LIMITS = pltpu.CompilerParams(vmem_limit_bytes=13 * 2**20)


def tile_of(size, limit):
    best = size
    for tile in range(128, min(size, limit) + 1, 128):
        if size % tile == 0:
            best = tile
    return best


def positive_of(own, moved, bias):
    return jnp.maximum(own.astype(F32) + moved.astype(F32) + bias, 0.0)


def tied(value, *first):
    return lax.optimization_barrier((value, *first))[0]


def product(left, right, left_dim, right_dim):
    return lax.dot_general(
        left, right, (((left_dim,), (right_dim,)), ((), ())), preferred_element_type=F32
    )


def encode_body(place_ref, rows_ref, gain_ref, weight_ref, normed_ref, *rest):
    send_refs, half_ref = rest[:-1], rest[-1]
    blocks = place_ref.shape[0] - 1
    tokens, half = half_ref.shape
    size = tokens // blocks

    @pl.when(pl.program_id(0) == 0)
    def _():
        column = pl.multiple_of(place_ref[blocks] * half, 128)
        for b in range(blocks):
            start = pl.multiple_of(place_ref[b] * size, size)
            values = rows_ref[pl.ds(start, size), :].astype(F32)
            scaling = lax.rsqrt(jnp.mean(values * values, axis=-1, keepdims=True) + 1e-06)
            kept = slice(b * size, (b + 1) * size)
            normed_ref[kept, :] = (values * scaling * gain_ref[...]).astype(BF16)
            half_ref[kept, :] = normed_ref[kept, pl.ds(column, half)]

    part = product(half_ref[...], weight_ref[...].astype(BF16), 1, 0)
    span = tokens // len(send_refs)
    for c, send_ref in enumerate(send_refs):
        send_ref[...] = part[c * span : (c + 1) * span].astype(BF16)


def encode(place, rows, gain, weight):
    tokens, width = rows.shape
    half, feats = weight.shape
    tile = tile_of(feats, 512)
    size = tokens // CHUNKS
    return pl.pallas_call(
        encode_body,
        grid_spec=pltpu.PrefetchScalarGridSpec(
            num_scalar_prefetch=1,
            grid=(feats // tile,),
            in_specs=[
                pl.BlockSpec((tokens, width), lambda f, place: (0, 0)),
                pl.BlockSpec((1, width), lambda f, place: (0, 0)),
                pl.BlockSpec((half, tile), lambda f, place: (0, f)),
            ],
            out_specs=[pl.BlockSpec((tokens, width), lambda f, place: (0, 0))]
            + [pl.BlockSpec((size, tile), lambda f, place: (0, f))] * CHUNKS,
            scratch_shapes=[pltpu.VMEM((tokens, half), BF16)],
        ),
        out_shape=[jax.ShapeDtypeStruct((tokens, width), BF16)]
        + [jax.ShapeDtypeStruct((size, feats), BF16)] * CHUNKS,
        name="encode",
    )(place, rows, gain, weight)


def mlp_body(
    k_steps, rows_ref, gate_ref, up_ref, down_ref, near_ref, far_ref, gate_acc, up_acc, hidden
):
    step = pl.program_id(0)

    @pl.when(step == 0)
    def _():
        gate_acc[...] = product(rows_ref[...], gate_ref[...], 1, 0)
        up_acc[...] = product(rows_ref[...], up_ref[...], 1, 0)

    @pl.when((step > 0) & (step < k_steps))
    def _():
        gate_acc[...] += product(rows_ref[...], gate_ref[...], 1, 0)
        up_acc[...] += product(rows_ref[...], up_ref[...], 1, 0)

    @pl.when(step == k_steps - 1)
    def _():
        hidden[...] = (jax.nn.gelu(gate_acc[...], approximate=True) * up_acc[...]).astype(BF16)

    @pl.when(step >= k_steps)
    def _():
        target = product(hidden[...], down_ref[...], 1, 0).astype(BF16)
        size = target.shape[0] // (2 * CHUNKS)
        for c in range(CHUNKS):
            kept = slice(c * size, (c + 1) * size)
            near_ref[kept, :] = target[2 * c * size : (2 * c + 1) * size]
            far_ref[kept, :] = target[(2 * c + 1) * size : (2 * c + 2) * size]


def mlp(normed, gate, up, down):
    tokens, width = normed.shape
    inner = gate.shape[1]
    tile = tile_of(width, 768)
    steps = width // tile
    early = lambda i: jnp.minimum(i, steps - 1)
    late = lambda i: jnp.maximum(i - steps, 0)
    return pl.pallas_call(
        functools.partial(mlp_body, steps),
        grid=(2 * steps,),
        in_specs=[
            pl.BlockSpec((tokens, tile), lambda i: (0, early(i))),
            pl.BlockSpec((tile, inner), lambda i: (early(i), 0)),
            pl.BlockSpec((tile, inner), lambda i: (early(i), 0)),
            pl.BlockSpec((inner, tile), lambda i: (0, late(i))),
        ],
        out_specs=[pl.BlockSpec((tokens // 2, tile), lambda i: (0, late(i)))] * 2,
        out_shape=[jax.ShapeDtypeStruct((tokens // 2, width), BF16)] * 2,
        scratch_shapes=[
            pltpu.VMEM((tokens, inner), F32),
            pltpu.VMEM((tokens, inner), F32),
            pltpu.VMEM((tokens, inner), BF16),
        ],
        name="mlp",
    )(normed, gate, up, down)


def preload_body(source_ref, out_ref, sem):
    copy = pltpu.make_async_copy(source_ref, out_ref, sem)
    copy.start()
    copy.wait()


def preload(decoders):
    return pl.pallas_call(
        preload_body,
        in_specs=[pl.BlockSpec(memory_space=pl.ANY)],
        out_specs=pl.BlockSpec(memory_space=pltpu.VMEM),
        out_shape=pltpu.VMEM(decoders.shape, decoders.dtype),
        scratch_shapes=[pltpu.SemaphoreType.DMA],
        compiler_params=LIMITS,
        name="preload",
    )(decoders)


def decode_body(
    flags_ref,
    own_ref,
    moved_ref,
    bias_ref,
    weight_ref,
    near_ref,
    far_ref,
    act_ref,
    keep_ref,
    send_ref,
):
    slot = pl.program_id(0)
    slots = pl.num_programs(0)

    @pl.when((slot == 0) & (pl.program_id(1) == 0))
    def _():
        positive = positive_of(own_ref[...], moved_ref[...], bias_ref[...])
        act_ref[...] = (positive * positive).astype(BF16)

    live = flags_ref[slot].astype(F32)
    mine = flags_ref[slots + slot].astype(F32)
    tile = near_ref.shape[1]
    column = pl.multiple_of(pl.program_id(1) * tile, tile)
    recon = product(act_ref[...], weight_ref[slot, :, pl.ds(column, tile)], 1, 0) * live
    half = recon.shape[0] // 2
    keep_ref[0] = recon[:half] - near_ref[...].astype(F32) * mine
    send_ref[0] = (recon[half:] - far_ref[...].astype(F32) * mine).astype(BF16)


def decode(flags, own, moved, bias, decoders, targets, chunk):
    size, feats = own.shape
    slots, _, width = decoders.shape
    tile = tile_of(width, 768)
    whole = pl.BlockSpec((size, feats), lambda j, d, flags: (0, 0))
    part = pl.BlockSpec((1, size // 2, tile), lambda j, d, flags: (j, 0, d))
    return pl.pallas_call(
        decode_body,
        grid_spec=pltpu.PrefetchScalarGridSpec(
            num_scalar_prefetch=1,
            grid=(slots, width // tile),
            in_specs=[
                whole,
                whole,
                pl.BlockSpec((1, feats), lambda j, d, flags: (0, 0)),
                pl.BlockSpec(memory_space=pltpu.VMEM),
                pl.BlockSpec((size // 2, tile), lambda j, d, flags: (chunk, d)),
                pl.BlockSpec((size // 2, tile), lambda j, d, flags: (chunk, d)),
            ],
            out_specs=[whole, part, part],
        ),
        out_shape=[
            jax.ShapeDtypeStruct((size, feats), BF16),
            jax.ShapeDtypeStruct((slots, size // 2, width), F32),
            jax.ShapeDtypeStruct((slots, size // 2, width), BF16),
        ],
        compiler_params=LIMITS,
        name="decode",
    )(flags, own, moved, bias, decoders, *targets)


def spread_body(dest_ref, *refs):
    count = len(refs) - dest_ref.shape[0]
    for k, out_ref in enumerate(refs[count:]):
        total = refs[0][:, dest_ref[k]].astype(F32)
        for value_ref in refs[1:count]:
            total = total + value_ref[:, dest_ref[k]].astype(F32)
        out_ref[...] = total.astype(BF16)


def choose_body(dest_ref, yes_ref, no_ref, *out_refs):
    feat_n = len(out_refs)
    for k, out_ref in enumerate(out_refs):
        yes, no = yes_ref[:, dest_ref[k]], no_ref[:, dest_ref[k]]
        out_ref[...] = jnp.where(dest_ref[feat_n] > 0, yes, no)


def spread(body, dest, values, feat_n):
    rows, width = values[0].shape[-2:]
    groups = values[-1].shape[0]
    whole = pl.BlockSpec((groups, feat_n, rows, width), lambda i, dest: (0, 0, 0, 0))
    piece = pl.BlockSpec((groups, rows, width), lambda i, dest: (0, 0, 0))
    return pl.pallas_call(
        body,
        grid_spec=pltpu.PrefetchScalarGridSpec(
            num_scalar_prefetch=1,
            grid=(1,),
            in_specs=[whole] * len(values),
            out_specs=[piece] * feat_n,
        ),
        out_shape=[jax.ShapeDtypeStruct((groups, rows, width), BF16)] * feat_n,
        compiler_params=LIMITS,
    )(dest, *values)


def back_body(count, flags_ref, *refs):
    pieces, weight_ref = refs[:count], refs[count]
    err_ref, part_ref, send_ref = refs[count + 1 :]
    slots = err_ref.shape[0]

    @pl.when(pl.program_id(0) == 0)
    def _():
        blocks, _, rows, _ = pieces[0].shape
        for j in range(slots):
            live = flags_ref[j].astype(BF16)
            for i, piece_ref in enumerate(pieces):
                for z in range(blocks):
                    start = (i * blocks + z) * rows
                    came = flags_ref[2 * slots + z]
                    err_ref[j, start : start + rows, :] = piece_ref[came, j] * live

    tile = part_ref.shape[1]
    kept = pl.ds(pl.multiple_of(pl.program_id(0) * tile, tile), tile)
    part = product(err_ref[0], weight_ref[0, kept, :], 1, 1)
    for j in range(1, slots):
        part = part + product(err_ref[j], weight_ref[j, kept, :], 1, 1)
    part_ref[...] = part
    send_ref[...] = part.astype(BF16)


def back_product(flags, pieces, decoders):
    blocks, slots, rows, width = pieces[0].shape
    size = len(pieces) * blocks * rows
    feats = decoders.shape[1]
    tile = tile_of(feats, 512)
    return pl.pallas_call(
        functools.partial(back_body, len(pieces)),
        grid_spec=pltpu.PrefetchScalarGridSpec(
            num_scalar_prefetch=1,
            grid=(feats // tile,),
            in_specs=[pl.BlockSpec((blocks, slots, rows, width), lambda f, flags: (0, 0, 0, 0))]
            * len(pieces)
            + [pl.BlockSpec(memory_space=pltpu.VMEM)],
            out_specs=[
                pl.BlockSpec((slots, size, width), lambda f, flags: (0, 0, 0)),
                pl.BlockSpec((size, tile), lambda f, flags: (0, f)),
                pl.BlockSpec((size, tile), lambda f, flags: (0, f)),
            ],
        ),
        out_shape=[
            jax.ShapeDtypeStruct((slots, size, width), BF16),
            jax.ShapeDtypeStruct((size, feats), F32),
            jax.ShapeDtypeStruct((size, feats), BF16),
        ],
        compiler_params=LIMITS,
        name="back_product",
    )(flags, *pieces, decoders)


def dec_grad_body(*refs):
    acts, errs, out_ref = refs[:CHUNKS], refs[CHUNKS : 2 * CHUNKS], refs[-1]
    turned = [act_ref[...].T for act_ref in acts]
    for j in range(out_ref.shape[0]):
        total = product(turned[0], errs[0][j], 1, 0)
        for c in range(1, CHUNKS):
            total = total + product(turned[c], errs[c][j], 1, 0)
        out_ref[j] = total.astype(BF16)


def dec_grad_product(actives, errors):
    size, feats = actives[0].shape
    slots, _, width = errors[0].shape
    tile = tile_of(feats, 256)
    return pl.pallas_call(
        dec_grad_body,
        grid=(feats // tile,),
        in_specs=[pl.BlockSpec((size, tile), lambda f: (0, f))] * CHUNKS
        + [pl.BlockSpec((slots, size, width), lambda f: (0, 0, 0))] * CHUNKS,
        out_specs=pl.BlockSpec((slots, tile, width), lambda f: (0, f, 0)),
        out_shape=jax.ShapeDtypeStruct((slots, feats, width), BF16),
        compiler_params=LIMITS,
        name="dec_grad",
    )(*actives, *errors)


def enc_grad_body(parity_ref, rows_ref, bias_in_ref, *refs):
    parts, moved, own, seen = (refs[i * CHUNKS : (i + 1) * CHUNKS] for i in range(4))
    grad_ref, bias_ref = refs[-2:]
    grads = []
    bias = 0.0
    for c in range(CHUNKS):
        positive = positive_of(own[c][...], seen[c][...], bias_in_ref[...])
        d_pre = (parts[c][...] + moved[c][...].astype(F32)) * 2.0 * positive
        bias = bias + jnp.sum(d_pre, axis=0, keepdims=True)
        grads.append(d_pre.astype(BF16))
    bias_ref[...] = bias
    grad_ref[...] = product(rows_ref[...], jnp.concatenate(grads, axis=0), 0, 0)


def enc_grad_product(parity, normed, half, bias, parts, moved, own, seen):
    tokens = normed.shape[0]
    size, feats = parts[0].shape
    tile = tile_of(feats, 512)
    return pl.pallas_call(
        enc_grad_body,
        grid_spec=pltpu.PrefetchScalarGridSpec(
            num_scalar_prefetch=1,
            grid=(feats // tile,),
            in_specs=[
                pl.BlockSpec((tokens, half), lambda f, par: (0, par[0])),
                pl.BlockSpec((1, tile), lambda f, par: (0, f)),
            ]
            + [pl.BlockSpec((size, tile), lambda f, par: (0, f))] * (4 * CHUNKS),
            out_specs=[
                pl.BlockSpec((half, tile), lambda f, par: (0, f)),
                pl.BlockSpec((1, tile), lambda f, par: (0, f)),
            ],
        ),
        out_shape=[
            jax.ShapeDtypeStruct((half, feats), F32),
            jax.ShapeDtypeStruct((1, feats), F32),
        ],
        compiler_params=LIMITS,
        name="enc_grad",
    )(parity, normed, bias, *parts, *moved, *own, *seen)


def shards(
    residual,
    norm_gain,
    gate_weight,
    up_weight,
    down_weight,
    enc_weight,
    enc_bias,
    dec_weight,
    dec_bias,
):
    layers = lax.axis_size("layer")
    feat_n = lax.axis_size("feat")
    outer = layers // 2
    source = lax.axis_index("layer")
    parity = lax.axis_index("par")
    place_z = lax.axis_index("feat")
    slots = dec_weight.shape[2]
    _, tokens, width = residual.shape
    half_width = enc_weight.shape[1]
    size = tokens // CHUNKS
    rows_n = size // (layers * feat_n)

    def over_par(value):
        return lax.ppermute(value, "par", [(0, 1), (1, 0)])

    def over_layer(value, mask):
        return lax.ppermute(value, "layer", [(s, s ^ mask) for s in range(layers)])

    def over_feat(value, shift):
        return lax.ppermute(value, "feat", [(z, (z + shift) % feat_n) for z in range(feat_n)])

    index = jnp.arange(CHUNKS * layers, dtype=jnp.int32)
    table = index ^ (source % 2 * outer + source // 2)
    parity_arg = jnp.full((1,), parity, jnp.int32)
    place = jnp.concatenate([table, parity_arg])
    normed, *pre_send = encode(place, residual[0], norm_gain, enc_weight[0])
    pre_moved = []
    for c in range(CHUNKS):
        pre_moved.append(over_par(pre_send[c]))
    targets = mlp(normed, gate_weight[0], up_weight[0], down_weight[0])

    pairs = [(s * 2 + 1 - s % 2, (s ^ 1) * 2 + 1 - s % 2) for s in range(layers)]
    handed = lax.ppermute(targets[1], ("layer", "par"), pairs)

    slot_ids = jnp.arange(slots, dtype=jnp.int32)
    feat_ids = jnp.arange(feat_n, dtype=jnp.int32)
    outer_ids = jnp.arange(outer, dtype=jnp.int32)
    live = 2 * slot_ids + parity >= source
    mine = (slot_ids == source // 2) & (source % 2 == parity)
    came = (feat_ids - place_z) % feat_n
    flags = jnp.concatenate([live.astype(jnp.int32), mine.astype(jnp.int32), came])
    own_target = jnp.full((1,), source % 2 == parity, jnp.int32)
    dest = jnp.concatenate([(feat_ids + place_z) % feat_n, own_target])
    chosen = (slot_ids[None] == (outer_ids[:, None] ^ (source // 2))).astype(F32)
    bias_rows = jnp.stack(
        [
            lax.dynamic_index_in_dim(dec_bias, 2 * j + parity, 0, keepdims=False)
            for j in range(slots)
        ]
    )
    flags, dest, chosen, bias_rows, decoders, _ = lax.optimization_barrier(
        (flags, dest, chosen, bias_rows, dec_weight, targets[0])
    )
    decoders = preload(decoders[0, 0])

    actives = []
    spreads = []
    for c in range(CHUNKS):
        seen = pre_moved[c]
        if c:
            seen = tied(seen, leaving)
        active, keep, send = decode(flags, pre_send[c], seen, enc_bias, decoders, targets, c)
        actives.append(active)
        got = over_layer(send, 1)
        keep = keep.reshape(slots, outer * feat_n, rows_n, width)
        got = got.reshape(keep.shape)
        arrived = [keep, got]
        leaving = got
        for high in range(1, outer):
            there = slice(high * feat_n, (high + 1) * feat_n)
            leaving = (keep[:, there] + got[:, there].astype(F32)).astype(BF16)
            arrived.append(over_layer(leaving, 2 * high))
        spreads.append(spread(spread_body, dest[:feat_n], arrived, feat_n))
        if c == 0:
            chunks = (CHUNKS * outer, feat_n, rows_n, width)
            pair = (tied(handed, leaving).reshape(chunks), targets[0].reshape(chunks))
            moving = spread(choose_body, dest, pair, feat_n)
            target_moved = [over_feat(moving[k], k) for k in range(1, feat_n)]

    summed = moving[0].astype(F32)
    for part in target_moved:
        summed = summed + part.astype(F32)
    summed = summed.astype(BF16).reshape(CHUNKS, outer, rows_n, width)
    far_target = 0.0
    for high in range(outer):
        got = over_par(summed[:, high])
        if high:
            got = over_layer(got, 2 * high)
        far_target = far_target + chosen[high][:, None, None, None] * got[None].astype(F32)

    gathered = []
    for c in range(CHUNKS):
        came = [over_feat(spreads[c][k], k) for k in range(1, feat_n)]
        if c:
            came[0] = tied(came[0], error)
        total = spreads[c][0].astype(F32)
        for part in came:
            total = total + part.astype(F32)
        error = (total - far_target[:, c] + bias_rows[:, None]) * 0.0625
        error = error.astype(BF16)
        came = [over_feat(error, feat_n - k) for k in range(1, feat_n)]
        gathered.append(jnp.stack([error] + came))

    errors = []
    parts = []
    moved = []
    for c in range(CHUNKS):
        pieces = [gathered[c]]
        for high in range(1, outer):
            pieces.append(over_layer(gathered[c], 2 * high))
        pieces = pieces + [over_layer(piece, 1) for piece in pieces]
        error, part, send = back_product(flags, pieces, decoders)
        errors.append(error)
        parts.append(part)
        moved.append(over_par(send))
    dec_grad = dec_grad_product(actives, errors)
    enc_grad, bias_grad = enc_grad_product(
        parity_arg, normed, half_width, enc_bias, parts, moved, pre_send, pre_moved
    )
    return (enc_grad[None], bias_grad, dec_grad[None, None])


def solution(mesh):
    return jax.shard_map(
        shards,
        mesh=mesh,
        in_specs=(
            P("layer", None, None),
            P("layer", None),
            P("layer", None, ("feat", "par")),
            P("layer", None, ("feat", "par")),
            P("layer", ("feat", "par"), None),
            P("layer", "par", "feat"),
            P("layer", "feat"),
            P("layer", "par", None, "feat", None),
            P(),
        ),
        out_specs=(
            P("layer", "par", "feat"),
            P("layer", "feat"),
            P("layer", "par", None, "feat", None),
        ),
        check_vma=False,
    )
```

```python
import functools

import jax
import jax.numpy as jnp
from jax import lax
from jax.experimental import pallas as pl
from jax.experimental.pallas import tpu as pltpu
from jax.sharding import PartitionSpec as P


CHUNKS = 2
PARTS = 2
F32 = jnp.float32
BF16 = jnp.bfloat16
LIMITS = pltpu.CompilerParams(vmem_limit_bytes=13 * 2**20)


def tile_of(size, limit):
    best = size
    for tile in range(128, min(size, limit) + 1, 128):
        if size % tile == 0:
            best = tile
    return best


def positive_of(own, moved, bias):
    return jnp.maximum(own.astype(F32) + moved.astype(F32) + bias, 0.0)


def tied(value, *first):
    return lax.optimization_barrier((value, *first))[0]


def product(left, right, left_dim, right_dim):
    return lax.dot_general(
        left, right, (((left_dim,), (right_dim,)), ((), ())), preferred_element_type=F32
    )


def encode_body(place_ref, rows_ref, gain_ref, weight_ref, normed_ref, *rest):
    send_refs, half_ref = rest[:-1], rest[-1]
    blocks = place_ref.shape[0] - 1
    tokens, half = half_ref.shape
    size = tokens // blocks

    @pl.when(pl.program_id(0) == 0)
    def _():
        column = pl.multiple_of(place_ref[blocks] * half, 128)
        for b in range(blocks):
            start = pl.multiple_of(place_ref[b] * size, size)
            values = rows_ref[pl.ds(start, size), :].astype(F32)
            scaling = lax.rsqrt(jnp.mean(values * values, axis=-1, keepdims=True) + 1e-06)
            kept = slice(b * size, (b + 1) * size)
            normed_ref[kept, :] = (values * scaling * gain_ref[...]).astype(BF16)
            half_ref[kept, :] = normed_ref[kept, pl.ds(column, half)]

    part = product(half_ref[...], weight_ref[...].astype(BF16), 1, 0)
    span = tokens // len(send_refs)
    for c, send_ref in enumerate(send_refs):
        send_ref[...] = part[c * span : (c + 1) * span].astype(BF16)


def encode(place, rows, gain, weight):
    tokens, width = rows.shape
    half, feats = weight.shape
    tile = tile_of(feats, 1024)
    size = tokens // CHUNKS
    return pl.pallas_call(
        encode_body,
        grid_spec=pltpu.PrefetchScalarGridSpec(
            num_scalar_prefetch=1,
            grid=(feats // tile,),
            in_specs=[
                pl.BlockSpec((tokens, width), lambda f, place: (0, 0)),
                pl.BlockSpec((1, width), lambda f, place: (0, 0)),
                pl.BlockSpec((half, tile), lambda f, place: (0, f)),
            ],
            out_specs=[pl.BlockSpec((tokens, width), lambda f, place: (0, 0))]
            + [pl.BlockSpec((size, tile), lambda f, place: (0, f))] * CHUNKS,
            scratch_shapes=[pltpu.VMEM((tokens, half), BF16)],
        ),
        out_shape=[jax.ShapeDtypeStruct((tokens, width), BF16)]
        + [jax.ShapeDtypeStruct((size, feats), BF16)] * CHUNKS,
        name="encode",
    )(place, rows, gain, weight)


def mlp_body(
    k_steps,
    rows_ref,
    gate_ref,
    up_ref,
    down_ref,
    source_ref,
    near_ref,
    far_ref,
    decoders_ref,
    gate_acc,
    up_acc,
    hidden,
    sems,
):
    step = pl.program_id(0)

    copies = []
    parts = sems.shape[0] // source_ref.shape[0]
    span = source_ref.shape[1] // parts
    for i in range(sems.shape[0]):
        kept = pl.ds(i % parts * span, span)
        copy = pltpu.make_async_copy(
            source_ref.at[i // parts, kept], decoders_ref.at[i // parts, kept], sems.at[i]
        )
        copies.append(copy)
        pl.when(step == min(i, 2 * k_steps - 1))(copy.start)

    @pl.when(step == 0)
    def _():
        gate_acc[...] = product(rows_ref[...], gate_ref[...], 1, 0)
        up_acc[...] = product(rows_ref[...], up_ref[...], 1, 0)

    @pl.when((step > 0) & (step < k_steps))
    def _():
        gate_acc[...] += product(rows_ref[...], gate_ref[...], 1, 0)
        up_acc[...] += product(rows_ref[...], up_ref[...], 1, 0)

    @pl.when(step == k_steps - 1)
    def _():
        hidden[...] = (jax.nn.gelu(gate_acc[...], approximate=True) * up_acc[...]).astype(BF16)

    @pl.when(step >= k_steps)
    def _():
        target = product(hidden[...], down_ref[...], 1, 0).astype(BF16)
        size = target.shape[0] // (2 * CHUNKS)
        for c in range(CHUNKS):
            kept = slice(c * size, (c + 1) * size)
            near_ref[kept, :] = target[2 * c * size : (2 * c + 1) * size]
            far_ref[kept, :] = target[(2 * c + 1) * size : (2 * c + 2) * size]

    @pl.when(step == 2 * k_steps - 1)
    def _():
        for copy in copies:
            copy.wait()


def mlp(normed, gate, up, down, decoders):
    tokens, width = normed.shape
    inner = gate.shape[1]
    tile = tile_of(width, 768)
    steps = width // tile
    early = lambda i: jnp.minimum(i, steps - 1)
    late = lambda i: jnp.maximum(i - steps, 0)
    return pl.pallas_call(
        functools.partial(mlp_body, steps),
        grid=(2 * steps,),
        in_specs=[
            pl.BlockSpec((tokens, tile), lambda i: (0, early(i))),
            pl.BlockSpec((tile, inner), lambda i: (early(i), 0)),
            pl.BlockSpec((tile, inner), lambda i: (early(i), 0)),
            pl.BlockSpec((inner, tile), lambda i: (0, late(i))),
            pl.BlockSpec(memory_space=pl.ANY),
        ],
        out_specs=[pl.BlockSpec((tokens // 2, tile), lambda i: (0, late(i)))] * 2
        + [pl.BlockSpec(memory_space=pltpu.VMEM)],
        out_shape=[jax.ShapeDtypeStruct((tokens // 2, width), BF16)] * 2
        + [pltpu.VMEM(decoders.shape, decoders.dtype)],
        scratch_shapes=[
            pltpu.VMEM((tokens, inner), F32),
            pltpu.VMEM((tokens, inner), F32),
            pltpu.VMEM((tokens, inner), BF16),
            pltpu.SemaphoreType.DMA((2 * decoders.shape[0],)),
        ],
        compiler_params=pltpu.CompilerParams(vmem_limit_bytes=42 * 2**20),
        name="mlp",
    )(normed, gate, up, down, decoders)


def decode_body(
    flags_ref,
    own_ref,
    moved_ref,
    bias_ref,
    weight_ref,
    near_ref,
    far_ref,
    act_ref,
    keep_ref,
    send_ref,
):
    slot = pl.program_id(0)
    slots = pl.num_programs(0)

    @pl.when((slot == 0) & (pl.program_id(1) == 0))
    def _():
        positive = positive_of(own_ref[...], moved_ref[...], bias_ref[...])
        act_ref[...] = (positive * positive).astype(BF16)

    live = flags_ref[slot].astype(F32)
    mine = flags_ref[slots + slot].astype(F32)
    tile = near_ref.shape[1]
    column = pl.multiple_of(pl.program_id(1) * tile, tile)
    recon = product(act_ref[...], weight_ref[slot, :, pl.ds(column, tile)], 1, 0) * live
    half = recon.shape[0] // 2
    keep_ref[0] = recon[:half] - near_ref[...].astype(F32) * mine
    send_ref[0] = (recon[half:] - far_ref[...].astype(F32) * mine).astype(BF16)


def decode(flags, own, moved, bias, decoders, targets, chunk):
    size, feats = own.shape
    slots, _, width = decoders.shape
    tile = tile_of(width, 768)
    whole = pl.BlockSpec((size, feats), lambda j, d, flags: (0, 0))
    part = pl.BlockSpec((1, size // 2, tile), lambda j, d, flags: (j, 0, d))
    return pl.pallas_call(
        decode_body,
        grid_spec=pltpu.PrefetchScalarGridSpec(
            num_scalar_prefetch=1,
            grid=(slots, width // tile),
            in_specs=[
                whole,
                whole,
                pl.BlockSpec((1, feats), lambda j, d, flags: (0, 0)),
                pl.BlockSpec(memory_space=pltpu.VMEM),
                pl.BlockSpec((size // 2, tile), lambda j, d, flags: (chunk, d)),
                pl.BlockSpec((size // 2, tile), lambda j, d, flags: (chunk, d)),
            ],
            out_specs=[whole, part, part],
        ),
        out_shape=[
            jax.ShapeDtypeStruct((size, feats), BF16),
            jax.ShapeDtypeStruct((slots, size // 2, width), F32),
            jax.ShapeDtypeStruct((slots, size // 2, width), BF16),
        ],
        compiler_params=LIMITS,
        name="decode",
    )(flags, own, moved, bias, decoders, *targets)


def spread_body(dest_ref, *refs):
    count = len(refs) - dest_ref.shape[0]
    for k, out_ref in enumerate(refs[count:]):
        total = refs[0][:, dest_ref[k]].astype(F32)
        for value_ref in refs[1:count]:
            total = total + value_ref[:, dest_ref[k]].astype(F32)
        out_ref[...] = total.astype(BF16)


def choose_body(dest_ref, yes_ref, no_ref, *out_refs):
    feat_n = len(out_refs)
    for k, out_ref in enumerate(out_refs):
        yes, no = yes_ref[:, dest_ref[k]], no_ref[:, dest_ref[k]]
        out_ref[...] = jnp.where(dest_ref[feat_n] > 0, yes, no)


def spread(body, dest, values, feat_n):
    rows, width = values[0].shape[-2:]
    groups = values[-1].shape[0]
    whole = pl.BlockSpec((groups, feat_n, rows, width), lambda i, dest: (0, 0, 0, 0))
    piece = pl.BlockSpec((groups, rows, width), lambda i, dest: (0, 0, 0))
    return pl.pallas_call(
        body,
        grid_spec=pltpu.PrefetchScalarGridSpec(
            num_scalar_prefetch=1,
            grid=(1,),
            in_specs=[whole] * len(values),
            out_specs=[piece] * feat_n,
        ),
        out_shape=[jax.ShapeDtypeStruct((groups, rows, width), BF16)] * feat_n,
        compiler_params=LIMITS,
    )(dest, *values)


def back_body(base, count, flags_ref, *refs):
    pieces, weight_ref, outs = refs[:count], refs[count], refs[count + 1 :]
    if count > 1:
        err_ref, part_ref, send_ref = outs
        slots = err_ref.shape[0]

        @pl.when(pl.program_id(0) == 0)
        def _():
            blocks, _, rows, _ = pieces[0].shape
            for j in range(slots):
                live = flags_ref[j].astype(BF16)
                for i, piece_ref in enumerate(pieces):
                    for z in range(blocks):
                        start = (i * blocks + z) * rows
                        came = flags_ref[2 * slots + z]
                        err_ref[j, start : start + rows, :] = piece_ref[came, j] * live

    else:
        err_ref = pieces[0]
        part_ref, send_ref = outs
        slots = err_ref.shape[0]

    tile = part_ref.shape[1]
    kept = pl.ds(pl.multiple_of(base + pl.program_id(0) * tile, tile), tile)
    part = product(err_ref[0], weight_ref[0, kept, :], 1, 1)
    for j in range(1, slots):
        part = part + product(err_ref[j], weight_ref[j, kept, :], 1, 1)
    part_ref[...] = part
    send_ref[...] = part.astype(BF16)


def back_product(flags, pieces, decoders, base, span):
    slots, width = decoders.shape[0], decoders.shape[2]
    if len(pieces) > 1:
        size = len(pieces) * pieces[0].shape[0] * pieces[0].shape[2]
    else:
        size = pieces[0].shape[1]
    tile = tile_of(span, 512)
    errors = (slots, size, width)
    extra = int(len(pieces) > 1)
    whole = lambda shape: pl.BlockSpec(shape, lambda f, flags: (0,) * len(shape))
    part = pl.BlockSpec((size, tile), lambda f, flags: (0, f))
    return pl.pallas_call(
        functools.partial(back_body, base, len(pieces)),
        grid_spec=pltpu.PrefetchScalarGridSpec(
            num_scalar_prefetch=1,
            grid=(span // tile,),
            in_specs=[whole(piece.shape) for piece in pieces]
            + [pl.BlockSpec(memory_space=pltpu.VMEM)],
            out_specs=[whole(errors)] * extra + [part, part],
        ),
        out_shape=[jax.ShapeDtypeStruct(errors, BF16)] * extra
        + [jax.ShapeDtypeStruct((size, span), F32), jax.ShapeDtypeStruct((size, span), BF16)],
        compiler_params=LIMITS,
        name="back_product",
    )(flags, *pieces, decoders)


def dec_grad_body(*refs):
    acts, errs, out_ref = refs[:CHUNKS], refs[CHUNKS : 2 * CHUNKS], refs[-1]
    turned = [act_ref[...].T for act_ref in acts]
    for j in range(out_ref.shape[0]):
        total = product(turned[0], errs[0][j], 1, 0)
        for c in range(1, CHUNKS):
            total = total + product(turned[c], errs[c][j], 1, 0)
        out_ref[j] = total.astype(BF16)


def dec_grad_product(actives, errors):
    size, feats = actives[0].shape
    slots, _, width = errors[0].shape
    tile = tile_of(feats, 256)
    return pl.pallas_call(
        dec_grad_body,
        grid=(feats // tile,),
        in_specs=[pl.BlockSpec((size, tile), lambda f: (0, f))] * CHUNKS
        + [pl.BlockSpec((slots, size, width), lambda f: (0, 0, 0))] * CHUNKS,
        out_specs=pl.BlockSpec((slots, tile, width), lambda f: (0, f, 0)),
        out_shape=jax.ShapeDtypeStruct((slots, feats, width), BF16),
        compiler_params=LIMITS,
        name="dec_grad",
    )(*actives, *errors)


def enc_grad_body(parity_ref, rows_ref, bias_in_ref, *refs):
    parts, moved, own, seen = (refs[i * CHUNKS : (i + 1) * CHUNKS] for i in range(4))
    grad_ref, bias_ref = refs[-2:]
    grads = []
    bias = 0.0
    for c in range(CHUNKS):
        positive = positive_of(own[c][...], seen[c][...], bias_in_ref[...])
        d_pre = (parts[c][...] + moved[c][...].astype(F32)) * 2.0 * positive
        bias = bias + jnp.sum(d_pre, axis=0, keepdims=True)
        grads.append(d_pre.astype(BF16))
    bias_ref[...] = bias
    grad_ref[...] = product(rows_ref[...], jnp.concatenate(grads, axis=0), 0, 0)


def enc_grad_product(parity, normed, half, bias, parts, moved, own, seen, base, before):
    tokens = normed.shape[0]
    size, feats = own[0].shape
    span = parts[0].shape[1]
    tile = tile_of(span, 512)
    first = base // tile
    local = pl.BlockSpec((size, tile), lambda f, par: (0, f))
    wide = pl.BlockSpec((size, tile), lambda f, par: (0, first + f))
    values = [normed, bias, *parts, *moved, *own, *seen]
    in_specs = [
        pl.BlockSpec((tokens, half), lambda f, par: (0, par[0])),
        pl.BlockSpec((1, tile), lambda f, par: (0, first + f)),
    ]
    in_specs += [local] * (2 * CHUNKS) + [wide] * (2 * CHUNKS)
    aliases = {}
    if before is not None:
        values.append(before)
        in_specs.append(pl.BlockSpec(memory_space=pl.ANY))
        aliases = {len(values): 0}
    return pl.pallas_call(
        enc_grad_body,
        grid_spec=pltpu.PrefetchScalarGridSpec(
            num_scalar_prefetch=1,
            grid=(span // tile,),
            in_specs=in_specs,
            out_specs=[
                pl.BlockSpec((half, tile), lambda f, par: (0, first + f)),
                pl.BlockSpec((1, tile), lambda f, par: (0, f)),
            ],
        ),
        out_shape=[
            jax.ShapeDtypeStruct((half, feats), F32),
            jax.ShapeDtypeStruct((1, span), F32),
        ],
        input_output_aliases=aliases,
        compiler_params=LIMITS,
        name="enc_grad",
    )(parity, *values)


def shards(
    residual,
    norm_gain,
    gate_weight,
    up_weight,
    down_weight,
    enc_weight,
    enc_bias,
    dec_weight,
    dec_bias,
):
    layers = lax.axis_size("layer")
    feat_n = lax.axis_size("feat")
    outer = layers // 2
    source = lax.axis_index("layer")
    parity = lax.axis_index("par")
    place_z = lax.axis_index("feat")
    slots = dec_weight.shape[2]
    _, tokens, width = residual.shape
    half_width = enc_weight.shape[1]
    size = tokens // CHUNKS
    rows_n = size // (layers * feat_n)

    def over_par(value):
        return lax.ppermute(value, "par", [(0, 1), (1, 0)])

    def over_layer(value, mask):
        return lax.ppermute(value, "layer", [(s, s ^ mask) for s in range(layers)])

    def over_feat(value, shift):
        return lax.ppermute(value, "feat", [(z, (z + shift) % feat_n) for z in range(feat_n)])

    index = jnp.arange(CHUNKS * layers, dtype=jnp.int32)
    table = index ^ (source % 2 * outer + source // 2)
    parity_arg = jnp.full((1,), parity, jnp.int32)
    place = jnp.concatenate([table, parity_arg])
    normed, *pre_send = encode(place, residual[0], norm_gain, enc_weight[0])
    pre_moved = []
    for c in range(CHUNKS):
        pre_moved.append(over_par(pre_send[c]))
    slot_ids = jnp.arange(slots, dtype=jnp.int32)
    feat_ids = jnp.arange(feat_n, dtype=jnp.int32)
    outer_ids = jnp.arange(outer, dtype=jnp.int32)
    live = 2 * slot_ids + parity >= source
    mine = (slot_ids == source // 2) & (source % 2 == parity)
    came = (feat_ids - place_z) % feat_n
    flags = jnp.concatenate([live.astype(jnp.int32), mine.astype(jnp.int32), came])
    own_target = jnp.full((1,), source % 2 == parity, jnp.int32)
    dest = jnp.concatenate([(feat_ids + place_z) % feat_n, own_target])
    chosen = (slot_ids[None] == (outer_ids[:, None] ^ (source // 2))).astype(F32)
    bias_rows = jnp.stack(
        [
            lax.dynamic_index_in_dim(dec_bias, 2 * j + parity, 0, keepdims=False)
            for j in range(slots)
        ]
    )
    flags, dest, chosen, bias_rows, normed = lax.optimization_barrier(
        (flags, dest, chosen, bias_rows, normed)
    )
    *targets, decoders = mlp(
        normed, gate_weight[0], up_weight[0], down_weight[0], dec_weight[0, 0]
    )

    pairs = [(s * 2 + 1 - s % 2, (s ^ 1) * 2 + 1 - s % 2) for s in range(layers)]
    handed = lax.ppermute(targets[1], ("layer", "par"), pairs)

    pair = (CHUNKS * outer, feat_n, rows_n, width)
    pair = (handed.reshape(pair), targets[0].reshape(pair))
    moving = spread(choose_body, dest, pair, feat_n)
    target_moved = [over_feat(moving[k], k) for k in range(1, feat_n)]

    actives = []
    spreads = []
    for c in range(CHUNKS):
        seen = pre_moved[c]
        if c:
            seen = tied(seen, leaving)
        active, keep, send = decode(flags, pre_send[c], seen, enc_bias, decoders, targets, c)
        actives.append(active)
        got = over_layer(send, 1)
        keep = keep.reshape(slots, outer * feat_n, rows_n, width)
        got = got.reshape(keep.shape)
        arrived = [keep, got]
        leaving = got
        for high in range(1, outer):
            there = slice(high * feat_n, (high + 1) * feat_n)
            leaving = (keep[:, there] + got[:, there].astype(F32)).astype(BF16)
            arrived.append(over_layer(leaving, 2 * high))
        spreads.append(spread(spread_body, dest[:feat_n], arrived, feat_n))

    summed = moving[0].astype(F32)
    for part in target_moved:
        summed = summed + part.astype(F32)
    summed = summed.astype(BF16).reshape(CHUNKS, outer, rows_n, width)
    far_target = 0.0
    for high in range(outer):
        pairs = [(s * 2 + p, (s ^ 2 * high) * 2 + 1 - p) for s in range(layers) for p in range(2)]
        got = lax.ppermute(summed[:, high], ("layer", "par"), pairs)
        far_target = far_target + chosen[high][:, None, None, None] * got[None].astype(F32)

    gathered = []
    for c in range(CHUNKS):
        came = [over_feat(spreads[c][k], k) for k in range(1, feat_n)]
        if c:
            came[0] = tied(came[0], error)
        total = spreads[c][0].astype(F32)
        for part in came:
            total = total + part.astype(F32)
        error = (total - far_target[:, c] + bias_rows[:, None]) * 0.0625
        error = error.astype(BF16)
        came = [over_feat(error, feat_n - k) for k in range(1, feat_n)]
        gathered.append(jnp.stack([error] + came))

    span = enc_bias.shape[1] // PARTS
    errors = []
    parts = [[] for _ in range(PARTS)]
    moved = [[] for _ in range(PARTS)]
    for c in range(CHUNKS):
        pieces = [gathered[c]]
        for high in range(1, outer):
            pieces.append(over_layer(gathered[c], 2 * high))
        pieces = pieces + [over_layer(piece, 1) for piece in pieces]
        for h in range(PARTS):
            *error, part, send = back_product(flags, pieces, decoders, h * span, span)
            if error:
                errors += error
                pieces = error
            parts[h].append(part)
            moved[h].append(over_par(send))
    dec_grad = dec_grad_product(actives, errors)
    enc_grad = None
    bias_grads = []
    for h in range(PARTS):
        enc_grad, bias_grad = enc_grad_product(
            parity_arg,
            normed,
            half_width,
            enc_bias,
            parts[h],
            moved[h],
            pre_send,
            pre_moved,
            h * span,
            enc_grad,
        )
        bias_grads.append(bias_grad)
    bias_grad = jnp.concatenate(bias_grads, axis=1)
    return (enc_grad[None], bias_grad, dec_grad[None, None])


def solution(mesh):
    return jax.shard_map(
        shards,
        mesh=mesh,
        in_specs=(
            P("layer", None, None),
            P("layer", None),
            P("layer", None, ("feat", "par")),
            P("layer", None, ("feat", "par")),
            P("layer", ("feat", "par"), None),
            P("layer", "par", "feat"),
            P("layer", "feat"),
            P("layer", "par", None, "feat", None),
            P(),
        ),
        out_specs=(
            P("layer", "par", "feat"),
            P("layer", "feat"),
            P("layer", "par", None, "feat", None),
        ),
        check_vma=False,
    )
```
